32 devices in a mesh: groups: 2 (over y), win: 4 (over z), segment: 4 (over x, core).
Axes of the slice: x: 2, y: 2, z: 4, core: 2. Of those that a mesh axis runs over, the one named last changes fastest.
Arguments:
- fields: bfloat16 [8, 8, 64, 1536], P(('groups', 'segment'), None, 'win'), parts along dimension 0, may hold values from -12 to 12
- step_index: int32 [8], P(('groups', 'segment')), parts along dimension 0, may hold values from 0 to 31
- shift_flags: int32 [4], P('segment'), may hold values from 0 to 1, as said below
- norm_gains: float32 [4, 1536], P('segment'), may hold values from 0.5 to 2
- input_weight: bfloat16 [4, 1536, 2304], P('segment'), may hold values from -0.15625 to 0.15625
- output_weight: bfloat16 [4, 768, 1536], P('segment'), may hold values from -0.21875 to 0.21875
- step_table: float32 [32, 1536], replicated, may hold values from -6 to 6
- step_rate: float32 [32], replicated, may hold values from 0.25 to 1
Outputs:
- advanced: bfloat16 [8, 8, 64, 1536], P(('groups', 'segment'), None, 'win'), parts along dimension 0
The draws below stay inside these ranges and needn't reach their ends.
There are 2 independent parts, one for each index of `groups`. The reference program is written for one: setup_inputs(seed, part) draws one part's arguments, and reference() takes and returns one part's arrays. A program takes and returns all parts, laid end to end along the dimension named above; an argument that names none is the same for every part. Nothing has to cross between parts.
Inputs may be any that keep to these rules, and one draw needn't show every extreme that they name: `shift_flags`: each entry is 0 or 1, and at least one layer has 1.
All inputs are finite; a program needn't handle non-finite values.
Results may differ from the reference program's by a relative error of at most 0.014.
Values may be sent and summed in bfloat16 or wider, within the bound.
A program may use at most 64 MiB of HBM per device.

```python
import math
import jax
import jax.numpy as jnp
from jax import lax

D = 1536
HEADS = 6
HEAD_DIM = 128
WIN_ROWS = 8
WIN_COLS = 16
STEP_COUNT = 32
LAYERS = 4
SAMPLES = 4
LAT = 8
LON = 64


def draw_fields(key, part):
    first_key, second_key, third_key = jax.random.split(key, 3)
    column_scale = jnp.exp(jax.random.uniform(second_key, (D,), jnp.float32, -1.15, 1.15))
    row_scale = jnp.exp(jax.random.uniform(third_key, (SAMPLES, LAT, LON, 1), jnp.float32, -1.15, 1.15))
    values = jax.random.normal(first_key, (SAMPLES, LAT, LON, D), jnp.float32) * column_scale * row_scale
    return jnp.clip(values, -12.0, 12.0).astype(jnp.bfloat16)


def draw_shift_flags(key, part):
    first_key, second_key = jax.random.split(jax.random.fold_in(key, 17), 2)
    random_bits = jax.random.randint(first_key, (LAYERS,), 0, 2)
    chosen = jax.random.randint(second_key, (), 0, LAYERS)
    return jnp.where(jnp.arange(LAYERS) == chosen, 1, random_bits).astype(jnp.int32)


def plant(drawn, key, low, largest):
    longest = drawn.shape.index(max(drawn.shape))
    spots = []
    for shift in (0, 1):
        where = [jax.random.randint(jax.random.fold_in(key, axis), (), 0, length) for axis, length in enumerate(drawn.shape)]
        where[longest] = (where[longest] + shift) % drawn.shape[longest]
        spots.append(tuple(where))
    return drawn.at[spots[0]].set(low).at[spots[1]].set(largest)


def steps_of(stream_key, shape, pieces, least, largest):
    loudness, own = 1.0, jax.random.fold_in(stream_key, 6)
    for axis_at, parts in pieces:
        heights = jnp.exp(jax.random.uniform(jax.random.fold_in(own, axis_at), (parts,), jnp.float32, least / len(pieces), largest / len(pieces)))
        loudness = loudness * jnp.repeat(heights, shape[axis_at] // parts).reshape([-1 if axis == axis_at else 1 for axis in range(len(shape))])
    return loudness


def centred(own_key, extent, scale, most, pieces=(), held_as=jnp.bfloat16):
    result = jax.random.normal(own_key, extent, jnp.float32) * scale
    if len(pieces) > 0:
        result = steps_of(own_key, extent, pieces, -0.22, 0.18) * result
    return jnp.clip(result, min=-most, max=most).astype(held_as)


def setup_inputs(seed: int = 0, part: int = 0) -> dict:
    streams_of = jax.random.split(jax.random.key(seed), 9)
    own_keys = jax.random.split(jax.random.fold_in(streams_of[8], part), 9)
    fields = draw_fields(jax.random.fold_in(jax.random.fold_in(streams_of[8], part), 71), part)
    step_index = plant(jax.random.randint(own_keys[1], (SAMPLES,), 0, STEP_COUNT), jax.random.fold_in(own_keys[1], 1), 0, STEP_COUNT - 1).astype(jnp.int32)
    shift_flags = draw_shift_flags(jax.random.fold_in(streams_of[8], 71), part)
    norm_gains = jnp.clip(jnp.exp(math.log(2.0) - 1.3862944 * jax.random.uniform(streams_of[3], (LAYERS, D), jnp.float32) ** steps_of(streams_of[3], (LAYERS, D), ((0, 4),), -0.2, 0.2)), 0.5, 2.0)
    input_weight = centred(streams_of[4], (LAYERS, D, 3 * HEADS * HEAD_DIM), D ** -0.5, 0.15625, ((0, 4),))
    output_weight = centred(streams_of[5], (LAYERS, HEADS * HEAD_DIM, D), (HEADS * HEAD_DIM) ** -0.5, 0.21875, ((0, 4),))
    step_table = centred(streams_of[6], (STEP_COUNT, D), 1.0, 6.0, (), jnp.float32)
    step_rate = jnp.clip(jnp.exp(jax.random.uniform(streams_of[7], (STEP_COUNT,), jnp.float32, math.log(0.25), math.log(1.0))), 0.25, 1.0)
    return {"fields": fields, "step_index": step_index, "shift_flags": shift_flags, "norm_gains": norm_gains, "input_weight": input_weight, "output_weight": output_weight, "step_table": step_table, "step_rate": step_rate}


def rms_scale(hidden, gain_row):
    mean_square = lax.optimization_barrier(jnp.mean(hidden * hidden, axis=-1, keepdims=True))
    return (hidden * lax.rsqrt(mean_square + 1e-06) * gain_row).astype(jnp.bfloat16)

def window_attention(normed, first_weight, second_weight):
    samples, lat_rows, lon_cols, feature_width = normed.shape
    inner_width = HEADS * HEAD_DIM
    bands = lat_rows // WIN_ROWS
    columns = lon_cols // WIN_COLS
    projected = jnp.dot(normed.reshape(-1, feature_width), first_weight, preferred_element_type=jnp.float32).astype(jnp.bfloat16)
    projected = projected.reshape(samples, bands, WIN_ROWS, columns, WIN_COLS, 3, HEADS, HEAD_DIM)
    projected = projected.transpose(0, 1, 3, 2, 4, 5, 6, 7).reshape(samples, bands, columns, WIN_ROWS * WIN_COLS, 3, HEADS, HEAD_DIM)
    queries = projected[:, :, :, :, 0].astype(jnp.float32)
    keys_all = projected[:, :, :, :, 1].astype(jnp.float32)
    values_all = projected[:, :, :, :, 2].astype(jnp.float32)
    scores = jnp.einsum('abcqhe,abckhe->abchqk', queries, keys_all) / math.sqrt(HEAD_DIM)
    weights = jnp.exp(scores)
    weights = (weights / lax.optimization_barrier(jnp.sum(weights, axis=-1, keepdims=True))).astype(jnp.bfloat16)
    heads = jnp.einsum('abchqk,abckhe->abcqhe', weights.astype(jnp.float32), values_all).astype(jnp.bfloat16)
    heads = heads.reshape(samples, bands, columns, WIN_ROWS, WIN_COLS, inner_width)
    heads = heads.transpose(0, 1, 3, 2, 4, 5).reshape(-1, inner_width)
    branch = jnp.dot(heads, second_weight, preferred_element_type=jnp.float32).astype(jnp.bfloat16)
    return branch.reshape(samples, lat_rows, lon_cols, feature_width)

def reference(fields, step_index, shift_flags, norm_gains, input_weight, output_weight, step_table, step_rate):
    half = WIN_COLS // 2
    start_field = (fields.astype(jnp.float32) + step_table[step_index][:, None, None, :]).astype(jnp.bfloat16)
    hidden = start_field
    for layer_index in range(LAYERS):
        normed = rms_scale(hidden.astype(jnp.float32), norm_gains[layer_index])
        shifted = shift_flags[layer_index] > 0
        rolled = jnp.where(shifted, jnp.roll(normed, -half, axis=2), normed)
        branch = window_attention(rolled, input_weight[layer_index], output_weight[layer_index])
        branch = jnp.where(shifted, jnp.roll(branch, half, axis=2), branch)
        hidden = (hidden.astype(jnp.float32) + branch.astype(jnp.float32)).astype(jnp.bfloat16)
    velocity = hidden.astype(jnp.float32) - start_field.astype(jnp.float32)
    step_size = step_rate[step_index][:, None, None, None]
    return (fields.astype(jnp.float32) + step_size * velocity).astype(jnp.bfloat16)
```

```python
import functools
import math

import jax
import jax.numpy as jnp
from jax import lax
from jax.experimental import pallas as pl
from jax.experimental.pallas import tpu as pltpu
from jax.sharding import PartitionSpec as P

HEADS = 6
TILE = 256
MESH = pl.DeviceIdType.MESH


def pick(table, index):
    value = table[0]
    for at, entry in enumerate(table[1:], 1):
        value = jnp.where(index == at, entry, value)
    return value


def kernel(
    segments,
    windows,
    index_ref,
    flag_ref,
    rate_ref,
    fields_ref,
    table_ref,
    gain_ref,
    first_hbm,
    second_hbm,
    advanced_ref,
    first_weight,
    second_weight,
    start,
    inbox,
    outbox,
    returned,
    entry_relay,
    home_relay,
    normed,
    projected,
    heads,
    weight_sem,
    start_send,
    inbox_sem,
    outbox_sem,
    return_sem,
    entry_relay_recv,
    entry_relay_send,
    home_relay_recv,
    home_relay_send,
    turn,
):
    seg = lax.axis_index("segment")
    win = lax.axis_index("win")
    stride = windows // segments
    working = lax.rem(win, stride) == 0
    spread = sorted(range(segments), key=lambda at: abs(2 * at + 1 - segments))
    column_of = [at * stride for at in spread]
    lower = segments // 2
    step_of = [
        1 if (2 * column + 1 > windows) == (owner >= lower) else -1
        for owner, column in enumerate(column_of)
    ]
    sample = pick([spread.index(at) for at in range(segments)], win // stride)

    def place(owner):
        if isinstance(owner, int):
            return column_of[owner], step_of[owner]
        return pick(column_of, owner), pick(step_of, owner)

    def slot_of(owner, chunk):
        column, step = place(owner)
        return lax.rem(step * (chunk - column) + 1 + 2 * windows, windows)

    def home_chunk(owner, slot):
        column, step = place(owner)
        turns = lax.rem(slot + segments // 2 - 1 + windows, windows)
        return lax.rem(column + step * turns + windows, windows)

    def entry_relayed(owner, chunk):
        column, _ = place(owner)
        distance = jnp.abs(chunk - column)
        return (owner >= lower) & (distance > 0) & (2 * distance <= windows)

    def home_relayed(owner, column, chunk):
        return (owner < lower) & ((2 * chunk >= windows) != (2 * column >= windows))

    half_tokens = start.shape[0] // 2
    lat_rows, cols, width = fields_ref.shape
    half = cols // 2
    inner_width = second_weight.shape[0]
    head_size = inner_width // HEADS
    last_layer = seg == segments - 1

    first_copy = pltpu.make_async_copy(first_hbm, first_weight, weight_sem.at[0])
    second_copy = pltpu.make_async_copy(second_hbm, second_weight, weight_sem.at[1])

    @pl.when(working)
    def _():
        first_copy.start()
        second_copy.start()

    barrier = pltpu.get_barrier_semaphore()
    count = segments * windows
    me = seg * windows + win

    @pl.loop(1, count)
    def _(step):
        other = lax.rem(me + step, count)
        pl.semaphore_signal(
            barrier,
            inc=1,
            device_id={"segment": other // windows, "win": lax.rem(other, windows)},
            device_id_type=MESH,
        )

    entry, step_here = place(seg)

    def columns(side):
        at = jnp.where(step_here > 0, side * half, (1 - side) * half)
        return pl.ds(pl.multiple_of(at, half), half)

    step_index = index_ref[0]
    offset_row = table_ref[pl.ds(step_index, 1), :]
    for side in range(2):
        piece = fields_ref[:, columns(side), :].astype(jnp.float32)
        piece = piece.reshape(half_tokens, width) + offset_row
        start[side * half_tokens : (side + 1) * half_tokens, :] = piece.astype(jnp.bfloat16)

    pl.semaphore_wait(barrier, count - 1)

    entry_slot = slot_of(seg, win)
    entry_by_relay = entry_relayed(seg, win)
    relays_home = working & (sample == seg) & (seg < lower)
    stays = (seg == 0) & (win == entry)
    goes_home = (seg == segments - 1) & working & (sample == seg)

    pair = seg + 1 - 2 * lax.rem(seg, 2)
    lead = slot_of(pair, win) - entry_slot
    gives = 2 * lead > windows
    yields = -2 * lead > windows

    start_copy = pltpu.make_async_remote_copy(
        src_ref=start,
        dst_ref=inbox.at[entry_slot],
        send_sem=start_send,
        recv_sem=inbox_sem.at[entry_slot],
        device_id={"segment": 0, "win": entry},
        device_id_type=MESH,
    )

    @pl.when(stays)
    def _():
        inbox[entry_slot] = start[...]

    start_relay = pltpu.make_async_remote_copy(
        src_ref=start,
        dst_ref=entry_relay.at[jnp.maximum(seg - lower, 0)],
        send_sem=start_send,
        recv_sem=entry_relay_recv.at[jnp.maximum(seg - lower, 0)],
        device_id={"segment": 1},
        device_id_type=MESH,
    )

    @pl.when(yields)
    def _():
        pl.semaphore_wait(turn, 1)

    @pl.when(entry_by_relay)
    def _():
        start_relay.start()

    @pl.when(jnp.logical_not(stays) & jnp.logical_not(entry_by_relay))
    def _():
        start_copy.start()

    @pl.when(gives)
    def _():
        @pl.when(jnp.logical_not(stays))
        def _():
            start_copy.wait_send()

        pl.semaphore_signal(turn, inc=1, device_id={"segment": pair}, device_id_type=MESH)

    def entry_forward(owner):
        slot = slot_of(owner, win)
        return pltpu.make_async_remote_copy(
            src_ref=entry_relay.at[owner - lower],
            dst_ref=inbox.at[slot],
            send_sem=entry_relay_send.at[owner - lower],
            recv_sem=inbox_sem.at[slot],
            device_id={"segment": 0, "win": column_of[owner]},
            device_id_type=MESH,
        )

    def entry_pass(owner):
        @pl.when((seg == 1) & entry_relayed(owner, win))
        def _():
            pltpu.make_async_remote_copy(
                src_ref=start,
                dst_ref=entry_relay.at[owner - lower],
                send_sem=start_send,
                recv_sem=entry_relay_recv.at[owner - lower],
                device_id={"segment": 0},
                device_id_type=MESH,
            ).wait_recv()
            entry_forward(owner).start()

    low_half = 2 * win < windows

    @pl.when(low_half)
    def _():
        for owner in sorted(range(lower, segments), key=lambda at: column_of[at]):
            entry_pass(owner)

    @pl.when(jnp.logical_not(low_half))
    def _():
        for owner in sorted(range(lower, segments), key=lambda at: -column_of[at]):
            entry_pass(owner)

    def arrival(slot):
        return pltpu.make_async_remote_copy(
            src_ref=start,
            dst_ref=inbox.at[slot],
            send_sem=start_send,
            recv_sem=inbox_sem.at[slot],
            device_id={"segment": 0, "win": entry},
            device_id_type=MESH,
        )

    def onward(slot):
        return pltpu.make_async_remote_copy(
            src_ref=outbox.at[slot],
            dst_ref=inbox.at[slot],
            send_sem=outbox_sem.at[slot],
            recv_sem=inbox_sem.at[slot],
            device_id={"segment": lax.rem(seg + 1, segments)},
            device_id_type=MESH,
        )

    def homeward(slot):
        return pltpu.make_async_remote_copy(
            src_ref=outbox.at[slot],
            dst_ref=returned,
            send_sem=outbox_sem.at[slot],
            recv_sem=return_sem,
            device_id={"segment": sample, "win": home_chunk(sample, slot)},
            device_id_type=MESH,
        )

    def home_through(slot):
        return pltpu.make_async_remote_copy(
            src_ref=outbox.at[slot],
            dst_ref=home_relay.at[slot],
            send_sem=outbox_sem.at[slot],
            recv_sem=home_relay_recv.at[slot],
            device_id={"segment": sample},
            device_id_type=MESH,
        )

    def home_forward(slot):
        return pltpu.make_async_remote_copy(
            src_ref=home_relay.at[slot],
            dst_ref=returned,
            send_sem=home_relay_send.at[slot],
            recv_sem=return_sem,
            device_id={"win": home_chunk(sample, slot)},
            device_id_type=MESH,
        )

    @pl.when(working)
    def _():
        shift = jnp.where(flag_ref[0] > 0, 1, 0)
        straddle = jnp.where(lax.rem(seg, 2) == 0, shift, 1 - shift)
        halves = 2 * windows

        def project(slot):
            gain_row = gain_ref[...]
            value = inbox[slot].astype(jnp.float32)
            mean_square = jnp.mean(value * value, axis=-1, keepdims=True)
            scale = lax.rsqrt(mean_square + 1e-06)
            normed[...] = (value * gain_row).astype(jnp.bfloat16)
            for at in range(0, 3 * inner_width, TILE):
                part = jnp.dot(
                    normed[...], first_weight[:, at : at + TILE], preferred_element_type=jnp.float32
                )
                part = (part * scale).astype(jnp.bfloat16)
                projected[2 * slot, :, at : at + TILE] = part[:half_tokens]
                projected[2 * slot + 1, :, at : at + TILE] = part[half_tokens:]

        def attend(unit):
            left = jnp.where(unit == 0, 0, lax.rem(2 * unit + halves - straddle, halves))
            right = lax.rem(left + 1, halves)

            def block(at):
                part = pl.ds(at, head_size)
                return jnp.concatenate([projected[left, :, part], projected[right, :, part]], axis=0)

            starts = range(0, inner_width, head_size)
            scores = [
                lax.dot_general(
                    block(at),
                    block(inner_width + at),
                    (((1,), (1,)), ((), ())),
                    preferred_element_type=jnp.float32,
                )
                for at in starts
            ]
            weights = [jnp.exp(score * (1.0 / math.sqrt(head_size))) for score in scores]
            totals = [jnp.sum(weight, axis=-1, keepdims=True) for weight in weights]
            weights = [
                (weight * (1.0 / total)).astype(jnp.bfloat16)
                for weight, total in zip(weights, totals)
            ]
            mixed = [
                jnp.dot(
                    weight, block(2 * inner_width + at), preferred_element_type=jnp.float32
                ).astype(jnp.bfloat16)
                for weight, at in zip(weights, starts)
            ]
            for at, mix in zip(starts, mixed):
                heads[2 * unit, :, at : at + head_size] = mix[:half_tokens]
                heads[2 * unit + 1, :, at : at + head_size] = mix[half_tokens:]

        def emit(slot):
            later = lax.rem(slot + 1, windows)
            first = 2 * slot + 1 + straddle
            own = jnp.concatenate([heads[first], heads[first + 1]], axis=0)
            for at in range(0, width, TILE):
                branch = jnp.dot(
                    own, second_weight[:, at : at + TILE], preferred_element_type=jnp.float32
                ).astype(jnp.bfloat16)
                hidden = jnp.concatenate(
                    [
                        inbox[slot, half_tokens:, at : at + TILE],
                        inbox[later, :half_tokens, at : at + TILE],
                    ],
                    axis=0,
                )
                outbox[slot, :, at : at + TILE] = (
                    hidden.astype(jnp.float32) + branch.astype(jnp.float32)
                ).astype(jnp.bfloat16)

            @pl.when(jnp.logical_not(last_layer))
            def _():
                onward(slot).start()

            chunk = home_chunk(sample, slot)
            through = home_relayed(sample, win, chunk)

            @pl.when(last_layer & through)
            def _():
                home_through(slot).start()

            @pl.when(
                last_layer & jnp.logical_not(through) & jnp.logical_not(goes_home & (chunk == win))
            )
            def _():
                homeward(slot).start()

            @pl.when(goes_home & (chunk == win))
            def _():
                returned[...] = outbox[slot]

        first_copy.wait()
        second_copy.wait()

        @pl.loop(0, windows + 1)
        def _(step):
            @pl.when(step < windows)
            def _():
                @pl.when(jnp.logical_not(stays & (step == entry_slot)))
                def _():
                    arrival(step).wait_recv()

                project(step)

            attend(step)

            @pl.when(step > 0)
            def _():
                emit(step - 1)

    @pl.when(relays_home)
    def _():
        @pl.loop(0, windows)
        def _(slot):
            @pl.when(home_relayed(seg, win, home_chunk(sample, slot)))
            def _():
                home_through(slot).wait_recv()
                home_forward(slot).start()

    @pl.when(jnp.logical_not(goes_home))
    def _():
        homeward(0).wait_recv()

    rate = rate_ref[step_index]
    for side in range(2):
        fields_part = fields_ref[:, columns(side), :].astype(jnp.float32)
        rows = pl.ds(side * half_tokens, half_tokens)
        velocity = returned[rows, :].astype(jnp.float32) - start[rows, :].astype(jnp.float32)
        advanced_ref[:, columns(side), :] = (
            fields_part + rate * velocity.reshape(lat_rows, half, width)
        ).astype(jnp.bfloat16)

    @pl.when(jnp.logical_not(stays) & jnp.logical_not(gives))
    def _():
        start_copy.wait_send()

    for owner in range(lower, segments):

        @pl.when((seg == 1) & entry_relayed(owner, win))
        def _():
            entry_forward(owner).wait_send()

    @pl.when(relays_home)
    def _():
        @pl.loop(0, windows)
        def _(slot):
            @pl.when(home_relayed(seg, win, home_chunk(sample, slot)))
            def _():
                home_forward(slot).wait_send()

    @pl.when(working)
    def _():
        @pl.loop(0, windows)
        def _(slot):
            @pl.when(jnp.logical_not(goes_home & (home_chunk(sample, slot) == win)))
            def _():
                homeward(slot).wait_send()


def shards(
    fields, step_index, shift_flags, norm_gains, input_weight, output_weight, step_table, step_rate
):
    segments, windows = lax.axis_size("segment"), lax.axis_size("win")
    _, lat_rows, cols, width = fields.shape
    tokens = lat_rows * cols
    inner_width = output_weight.shape[1]
    smem = pl.BlockSpec(memory_space=pltpu.SMEM)
    vmem = pl.BlockSpec(memory_space=pltpu.VMEM)
    hbm = pl.BlockSpec(memory_space=pl.ANY)
    advanced = pl.pallas_call(
        functools.partial(kernel, segments, windows),
        out_shape=jax.ShapeDtypeStruct((lat_rows, cols, width), jnp.bfloat16),
        in_specs=[smem, smem, smem, vmem, vmem, vmem, hbm, hbm],
        out_specs=vmem,
        scratch_shapes=[
            pltpu.VMEM(input_weight.shape[1:], jnp.bfloat16),
            pltpu.VMEM(output_weight.shape[1:], jnp.bfloat16),
            pltpu.VMEM((tokens, width), jnp.bfloat16),
            pltpu.VMEM((windows, tokens, width), jnp.bfloat16),
            pltpu.VMEM((windows, tokens, width), jnp.bfloat16),
            pltpu.VMEM((tokens, width), jnp.bfloat16),
            pltpu.VMEM((segments - segments // 2, tokens, width), jnp.bfloat16),
            pltpu.VMEM((windows, tokens, width), jnp.bfloat16),
            pltpu.VMEM((tokens, width), jnp.bfloat16),
            pltpu.VMEM((2 * windows, tokens // 2, 3 * inner_width), jnp.bfloat16),
            pltpu.VMEM((2 * windows + 2, tokens // 2, inner_width), jnp.bfloat16),
            pltpu.SemaphoreType.DMA((2,)),
            pltpu.SemaphoreType.DMA,
            pltpu.SemaphoreType.DMA((windows,)),
            pltpu.SemaphoreType.DMA((windows,)),
            pltpu.SemaphoreType.DMA,
            pltpu.SemaphoreType.DMA((segments - segments // 2,)),
            pltpu.SemaphoreType.DMA((segments - segments // 2,)),
            pltpu.SemaphoreType.DMA((windows,)),
            pltpu.SemaphoreType.DMA((windows,)),
            pltpu.SemaphoreType.REGULAR,
        ],
        compiler_params=pltpu.CompilerParams(
            collective_id=0, has_side_effects=True, vmem_limit_bytes=60 * 1024 * 1024
        ),
    )(
        step_index,
        shift_flags,
        step_rate,
        fields[0],
        step_table,
        norm_gains,
        input_weight[0],
        output_weight[0],
    )
    return advanced[None]


def solution(mesh):
    return jax.shard_map(
        shards,
        mesh=mesh,
        in_specs=(
            P(("groups", "segment"), None, "win", None),
            P(("groups", "segment")),
            P("segment"),
            P("segment", None),
            P("segment", None, None),
            P("segment", None, None),
            P(),
            P(),
        ),
        out_specs=P(("groups", "segment"), None, "win", None),
        check_vma=False,
    )
```
